32 devices in a mesh: parts: 2 (over x), sub: 16 (over z, y, core).
Axes of the slice: x: 2, y: 2, z: 4, core: 2. Of those that a mesh axis runs over, the one named last changes fastest.
Arguments:
- right_side: float32 [32768, 256], P(('parts', 'sub')), parts along dimension 0, may hold values from -6 to 6
- face_weight: float32 [64, 512], P(('parts', 'sub')), parts along dimension 0, may hold values from 0.2 to 0.8
- schur: bfloat16 [65536, 1024], P(('parts', 'sub')), parts along dimension 0, as said below
- neumann: bfloat16 [65536, 1024], P(('parts', 'sub')), parts along dimension 0
- constraint: bfloat16 [2048, 512], P(('parts', 'sub')), parts along dimension 0, may hold values from -0.25 to 0.25
- coarse_inverse: bfloat16 [2048, 1024], P(('parts', 'sub')), parts along dimension 0
Outputs:
- solution: float32 [32768, 256], P(('parts', 'sub')), parts along dimension 0
- residual: float32 [32768, 256], P(('parts', 'sub')), parts along dimension 0
The draws below stay inside these ranges and needn't reach their ends.
There are 2 independent parts, one for each index of `parts`. The reference program is written for one: setup_inputs(seed, part) draws one part's arguments, and reference() takes and returns one part's arrays. A program takes and returns all parts, laid end to end along the dimension named above; each array names one. Nothing has to cross between parts.
Inputs may be any that keep to these rules, and one draw needn't show every extreme that they name: schur, neumann and coarse_inverse are symmetric, and each block schur_j, neumann_j and the whole coarse_inverse is positive definite.
All inputs are finite; a program needn't handle non-finite values.
Results may differ from the reference program's by a relative error of at most 0.0091.
Values may be sent and summed in bfloat16 or wider, within the bound.
A program may use at most 64 MiB of HBM per device.

```python
import math
import jax
import jax.numpy as jnp
from jax import lax

NF = 512
NCF = 32
R = 256
ITERS = 2
NI = 1024
SUBS = 32
NCO = 1024


def spd_block(key, matrix_order):
    first_key, second_key = jax.random.split(key)
    entries = jax.random.normal(first_key, (matrix_order, matrix_order), jnp.float32)
    diagonal = jax.random.uniform(second_key, (matrix_order,), jnp.float32, 1.0, 3.0)
    symmetric = (entries + entries.T) / (2.0 * math.sqrt(2.0 * matrix_order))
    return jnp.diag(diagonal) + 0.9 * symmetric


def spd_stack(key, salt):
    keys = jax.random.split(jax.random.fold_in(key, salt), SUBS)
    blocks = lax.map(lambda block_key: spd_block(block_key, NI), keys)
    return blocks.reshape(SUBS * NI, NI).astype(jnp.bfloat16)


def draw_schur(key, part):
    return spd_stack(key, 11)


def draw_neumann(key, part):
    return spd_stack(key, 23)


def draw_coarse_inverse(key, part):
    return spd_block(jax.random.fold_in(key, 37), NCO).astype(jnp.bfloat16)


def levels(rng, dims, shards, smallest, high):
    loudness = 1.0
    for dim, blocks in shards:
        steps = jax.random.uniform(jax.random.fold_in(jax.random.fold_in(rng, 6), dim), (blocks,), jnp.float32, smallest / len(shards), high / len(shards))
        loudness = loudness * jnp.repeat(jnp.exp(steps), dims[dim] // blocks).reshape((-1,) + (1,) * (len(dims) - 1 - dim))
    return loudness


def gaussian(own_key, dims, deviation, limit, cuts=(), dtype=jnp.bfloat16):
    array = jax.random.normal(own_key, dims, jnp.float32) * deviation
    if len(cuts) > 0:
        array = levels(own_key, dims, cuts, -0.22, 0.18) * array
    return jnp.clip(array, min=-limit, max=limit).astype(dtype)


def setup_inputs(seed: int = 0, part: int = 0) -> dict:
    key_list = jax.random.split(jax.random.key(seed), 7)
    own_keys = jax.random.split(jax.random.fold_in(key_list[6], part), 7)
    return {
        "right_side": gaussian(own_keys[0], (SUBS * NF, R), 1.0, 6.0, ((0, 16),), jnp.float32),
        "face_weight": jnp.clip(0.2 + 0.6 * jax.random.uniform(own_keys[1], (SUBS, NF), jnp.float32) ** levels(own_keys[1], (SUBS, NF), ((0, 16),), -0.2, 0.2), 0.2, 0.8),
        "schur": draw_schur(jax.random.fold_in(jax.random.fold_in(key_list[6], part), 71), part),
        "neumann": draw_neumann(jax.random.fold_in(jax.random.fold_in(key_list[6], part), 71), part),
        "constraint": gaussian(own_keys[4], (SUBS * NCF, NF), NF ** -0.5, 0.25, ((0, 16),)),
        "coarse_inverse": draw_coarse_inverse(jax.random.fold_in(jax.random.fold_in(key_list[6], part), 71), part),
    }


def couple(matrices, left_part, right_part):
    stacked = jnp.concatenate([left_part, right_part], axis=1)
    return lax.map(lambda operands: jnp.dot(operands[0], operands[1], preferred_element_type=jnp.float32), (matrices, stacked))


def schur_apply(blocks, vector):
    rounded = vector.astype(jnp.bfloat16)
    output = couple(blocks, jnp.roll(rounded, 1, axis=0), rounded)
    return output[:, NF:] + jnp.roll(output[:, :NF], -1, axis=0)


def neumann_apply(blocks, weights, vector):
    right_part = (weights * vector).astype(jnp.bfloat16)
    left_source = ((1.0 - weights) * vector).astype(jnp.bfloat16)
    output = couple(blocks, jnp.roll(left_source, 1, axis=0), right_part)
    return weights * output[:, NF:] + (1.0 - weights) * jnp.roll(output[:, :NF], -1, axis=0)


def precondition(neumann_blocks, weights, rows_constraint, coarse_inverse, vector):
    local_part = neumann_apply(neumann_blocks, weights, vector)
    rounded = vector.astype(jnp.bfloat16)
    coarse_input = jnp.einsum("jqf,jfr->jqr", rows_constraint.astype(jnp.float32), rounded.astype(jnp.float32)).astype(jnp.bfloat16)
    coarse_solution = jnp.dot(coarse_inverse, coarse_input.reshape(NCO, R), preferred_element_type=jnp.float32).astype(jnp.bfloat16)
    coarse_solution = coarse_solution.reshape(SUBS, NCF, R)
    correction = jnp.einsum("jqf,jqr->jfr", rows_constraint.astype(jnp.float32), coarse_solution.astype(jnp.float32))
    return local_part + correction


def reference(right_side, face_weight, schur, neumann, constraint, coarse_inverse):
    schur_blocks = schur.reshape(SUBS, NI, NI)
    neumann_blocks = neumann.reshape(SUBS, NI, NI)
    rows_constraint = constraint.reshape(SUBS, NCF, NF)
    weights = face_weight.reshape(SUBS, NF, 1)
    residual = right_side.reshape(SUBS, NF, R)
    solution = jnp.zeros_like(residual)
    precond = precondition(neumann_blocks, weights, rows_constraint, coarse_inverse, residual)
    direction = precond
    norm_now = jnp.sum(residual * precond, axis=(0, 1))
    for iteration in range(ITERS):
        product_image = schur_apply(schur_blocks, direction)
        step_size = norm_now / jnp.sum(direction * product_image, axis=(0, 1))
        solution = solution + step_size * direction
        residual = residual - step_size * product_image
        if iteration + 1 < ITERS:
            precond = precondition(neumann_blocks, weights, rows_constraint, coarse_inverse, residual)
            norm_next = jnp.sum(residual * precond, axis=(0, 1))
            direction = precond + (norm_next / norm_now) * direction
            norm_now = norm_next
    return solution.reshape(SUBS * NF, R), residual.reshape(SUBS * NF, R)
```

```python
import functools

import jax
import jax.numpy as jnp
from jax import lax
from jax.experimental import pallas as pl
from jax.experimental.pallas import tpu as pltpu
from jax.sharding import PartitionSpec as P

MESH = pl.DeviceIdType.MESH
STREAMS = 2
VMEM = 67043328
F32, BF16 = jnp.float32, jnp.bfloat16

INIT_P, N0_P, N0_Q, S0_P, S0_Q, N1_P, N1_Q, S1_Q = range(8)
MESSAGES = 8


def dot(a, b):
    return jnp.dot(a, b, preferred_element_type=F32)


def dot_first(a, b):
    return lax.dot_general(a, b, (((0,), (0,)), ((), ())), preferred_element_type=F32)


def column_sum(value):
    return jnp.sum(value, axis=0, keepdims=True)


def kernel(
    n, streams,
    rs_hbm, w_hbm, schur_hbm, neumann_hbm, con_hbm, ainv_hbm,
    sol_ref, out_ref,
    w, w_left, schur, neumann, con, ainv, wb,
    res, part, dirn, image, zed,
    sent, came, coarse0, coarse1, slots1, slots2,
    load_sem, aux_sem, msg_send, msg_recv, ag_sem, ar_sem,
):
    ls, nf = w_hbm.shape
    ni = schur_hbm.shape[1]
    ncf = con_hbm.shape[0] // ls
    cw = rs_hbm.shape[1] // streams
    me = lax.axis_index("sub")
    right, left = lax.rem(me + 1, n), lax.rem(me + n - 1, n)
    core, chip = lax.rem(me, 2), me // 2
    partner = chip * 2 + 1 - core

    rest, last = pl.ds(0, (ls - 1) * nf), pl.ds((ls - 1) * nf, nf)
    low, high = pl.ds(0, (ls - 1) * ni), pl.ds((ls - 1) * ni, ni)
    loads = [
        pltpu.make_async_copy(src, dst, load_sem.at[i])
        for i, (src, dst) in enumerate((
            (rs_hbm.at[last], res.at[pl.ds(ls * nf, nf)]),
            (rs_hbm.at[rest], res.at[pl.ds(nf, (ls - 1) * nf)]),
            (con_hbm, con.at[pl.ds(ncf, ls * ncf)]),
            (w_hbm, w),
            (neumann_hbm.at[high], neumann.at[high]),
            (neumann_hbm.at[low], neumann.at[low]),
            (ainv_hbm, ainv.at[pl.ds(ncf, ls * ncf)]),
            (schur_hbm, schur),
        ))
    ]
    for load in loads:
        load.start()

    barrier = pltpu.get_barrier_semaphore()

    def greet(k, carry):
        pl.semaphore_signal(barrier, inc=1, device_id={"sub": lax.rem(me + k, n)}, device_id_type=MESH)
        return carry

    lax.fori_loop(1, n, greet, 0)

    blocks = (coarse0, coarse1)

    def columns(st):
        return pl.ds(st * cw, cw)

    def face(f):
        return pl.ds(f * nf, nf)

    def message(st, m):
        to_right = m in (INIT_P, N0_P, S0_P, N1_P)
        return pltpu.make_async_remote_copy(
            src_ref=sent.at[st, m], dst_ref=came.at[st, m],
            send_sem=msg_send.at[st, m], recv_sem=msg_recv.at[st, m],
            device_id={"sub": right if to_right else left}, device_id_type=MESH,
        )

    def send(st, m, value):
        sent[st, m] = value.astype(BF16)
        message(st, m).start()

    def receive(st, m):
        message(st, m).wait_recv()
        return came[st, m].astype(F32)

    def gather_copy(inst, st, target):
        block = blocks[inst].at[st, chip, core]
        return pltpu.make_async_remote_copy(
            src_ref=block, dst_ref=block, send_sem=ag_sem.at[inst, st, 0], recv_sem=ag_sem.at[inst, st, 1],
            device_id={"sub": target}, device_id_type=MESH,
        )

    def gather_all(inst, st):
        most = blocks[inst].at[st, pl.ds(0, n // 2 - 1), core]
        return pltpu.make_async_remote_copy(
            src_ref=most, dst_ref=most, send_sem=ag_sem.at[inst, st, 0], recv_sem=ag_sem.at[inst, st, 1],
            device_id={"sub": partner}, device_id_type=MESH,
        )

    def gather_relay(inst, st, side):
        half = blocks[inst].at[st, :, side]
        return pltpu.make_async_remote_copy(
            src_ref=half, dst_ref=half, send_sem=ag_sem.at[inst, st, 2], recv_sem=ag_sem.at[inst, st, 3],
            device_id={"sub": partner}, device_id_type=MESH,
        )

    def restrict(st, vector, faces):
        return jnp.concatenate(
            [dot(con[pl.ds(f * ncf, ncf), :], vector[face(f), columns(st)].astype(BF16)) for f in faces], axis=0
        )

    def coarse_start(inst, st, value):
        blocks[inst][st, chip, core] = value.astype(BF16)

    def coarse_send(inst, st):
        def one(k, carry):
            gather_copy(inst, st, lax.rem(me + 2 * k, n)).start()
            return carry

        lax.fori_loop(1, n // 2, one, 0)

    def coarse_relay(inst, st):
        gather_all(inst, st).wait_recv()
        gather_relay(inst, st, core).start()

    def coarse_finish(inst, st):
        gather_relay(inst, st, 1 - core).wait_recv()
        return dot(ainv[...], blocks[inst][st].reshape(-1, cw))

    def reduce_copy(slots, inst, st, target):
        return pltpu.make_async_remote_copy(
            src_ref=slots.at[st, me], dst_ref=slots.at[st, me],
            send_sem=ar_sem.at[inst, st, 0], recv_sem=ar_sem.at[inst, st, 1],
            device_id={"sub": target}, device_id_type=MESH,
        )

    def reduce_most(slots, inst, st):
        most = slots.at[st, pl.ds(0, n - 1)]
        return pltpu.make_async_remote_copy(
            src_ref=most, dst_ref=most, send_sem=ar_sem.at[inst, st, 0], recv_sem=ar_sem.at[inst, st, 1],
            device_id={"sub": partner}, device_id_type=MESH,
        )

    def reduce_start(slots, inst, st, rows):
        slots[st, me] = jnp.concatenate(rows, axis=0)

        def one(k, carry):
            reduce_copy(slots, inst, st, lax.rem(me + k, n)).start()
            return carry

        lax.fori_loop(1, n, one, 0)

    def reduce_finish(slots, inst, st):
        reduce_most(slots, inst, st).wait_recv()
        return jnp.sum(slots[st], axis=0)

    def weighted(kind, f, k, value):
        if kind == "s":
            return value
        return value * (wb[f] if k == 1 else 1.0 - wb[f])

    def operand(st, kind, vector, s, ks):
        parts = [weighted(kind, s + k, k, vector[face(s + k), columns(st)]).astype(BF16) for k in ks]
        return parts[0] if len(parts) == 1 else jnp.concatenate(parts, axis=0)

    def product(kind, s, h, ks, value):
        matrix = neumann if kind == "n" else schur
        block = matrix[pl.ds(s * ni + h * nf, nf), pl.ds(ks[0] * nf, len(ks) * nf)]
        return dot(block, value)

    def early(st, kind, vector, late, m, before=None):
        cs = columns(st)
        order = list(range(ls)) if late == ls else list(range(ls - 1, -1, -1))
        seen = set()
        for s in order:
            if before is not None:
                before(s)
            ks = [k for k in (0, 1) if s + k != late]
            value = operand(st, kind, vector, s, ks)
            for h in (0, 1) if late == ls else (1, 0):
                f = s + h
                term = product(kind, s, h, ks, value)
                if f != late:
                    term = weighted(kind, f, h, term)
                if f in seen:
                    term = part[face(f), cs] + term
                part[face(f), cs] = term
                seen.add(f)
                if m is not None and f == ls - late:
                    send(st, m, term)

    def late_face(st, kind, vector, late, m):
        cs = columns(st)
        s, k = (0, 0) if late == 0 else (ls - 1, 1)
        value = operand(st, kind, vector, s, [k])
        for h in (k, 1 - k):
            f = s + h
            term = product(kind, s, h, [k], value)
            if f == late:
                term = weighted(kind, f, h, part[face(f), cs] + term)
            else:
                term = part[face(f), cs] + weighted(kind, f, h, term)
            part[face(f), cs] = term
            if m is not None and f == late:
                send(st, m, term)

    def inner(st, first, second, faces):
        total = None
        for f in faces:
            term = column_sum(first[face(f), columns(st)] * second[face(f), columns(st)])
            total = term if total is None else total + term
        return total

    every, owned = range(ls + 1), range(1, ls + 1)
    sts = range(streams)

    loads[0].wait()
    for st in sts:
        sent[st, INIT_P] = res[face(ls), columns(st)].astype(BF16)
    loads[1].wait()
    loads[2].wait()
    c32 = {st: restrict(st, res, owned) for st in sts}
    for st in sts:
        coarse_start(0, st, c32[st])
    pl.semaphore_wait(barrier, n - 1)

    last_rows = pl.ds((ls - 1) * ncf, ncf)
    aux = [
        pltpu.make_async_remote_copy(
            src_ref=src, dst_ref=dst, send_sem=aux_sem.at[i, 0], recv_sem=aux_sem.at[i, 1],
            device_id={"sub": right}, device_id_type=MESH,
        )
        for i, (src, dst) in enumerate((
            (w_hbm, w_left),
            (ainv_hbm.at[last_rows], ainv.at[pl.ds(0, ncf)]),
            (con_hbm.at[last_rows], con.at[pl.ds(0, ncf)]),
        ))
    ]
    for st in sts:
        message(st, INIT_P).start()
    aux[0].start()
    for st in sts:
        coarse_send(0, st)
    aux[1].start()
    aux[2].start()

    def spread(row):
        return jnp.transpose(jnp.broadcast_to(row, (cw, nf)))

    loads[3].wait()
    for f in range(ls):
        wb[f + 1] = spread(w[pl.ds(f, 1), :])
    loads[4].wait()

    def second_half(st, s):
        if st == 0 and s == ls - 2:
            loads[5].wait()

    def neumann_late(st, m):
        late_face(st, "n", res, 0, m)
        return inner(st, res, part, every)

    def schur_early(inst, st, target, p_message, q_message):
        cs = columns(st)
        x32 = coarse_finish(inst, st)
        if inst == 0:
            x0[st] = x32
        else:
            x32 = x0[st] - alpha0[st] * x32
        x = x32.astype(BF16)
        norm = column_sum(c32[st] * x[ncf:, :].astype(F32))
        for f in every:
            value = part[face(f), cs] + dot_first(con[pl.ds(f * ncf, ncf), :], x[f * ncf : (f + 1) * ncf, :])
            if f == 0:
                value = value + receive(st, p_message)
            target[face(f), cs] = value
        early(st, "s", target, ls, q_message)
        return norm

    def schur_late(st, target, q_arrived, p_message):
        cs = columns(st)
        target[face(ls), cs] = target[face(ls), cs] + receive(st, q_arrived)
        late_face(st, "s", target, ls, p_message)

    x0, alpha0, norm0, bent0, coupled, norm = {}, {}, {}, {}, {}, {}

    for st in sts:
        early(st, "n", res, 0, N0_P, functools.partial(second_half, st))
    aux[0].wait_recv()
    wb[0] = spread(w_left[pl.ds(ls - 1, 1), :])
    for st in sts:
        res[face(0), columns(st)] = receive(st, INIT_P)
        coupled[st] = neumann_late(st, N0_Q)
    coarse_relay(0, 0)
    loads[6].wait()
    aux[1].wait_recv()
    aux[2].wait_recv()
    loads[7].wait()
    for st in sts:
        norm[st] = coupled[st] + schur_early(0, st, dirn, N0_P, S0_Q)
        if st + 1 < streams:
            coarse_relay(0, st + 1)
    for st in sts:
        schur_late(st, dirn, N0_Q, S0_P)
        reduce_start(slots1, 0, st, [norm[st], inner(st, dirn, part, every)])
    for st in sts:
        cs = columns(st)
        for f in owned:
            value = part[face(f), cs]
            if f == ls:
                value = value + receive(st, S0_Q)
            image[face(f), cs] = value
        coarse_start(1, st, restrict(st, image, owned))
        coarse_send(1, st)
    for st in sts:
        cs = columns(st)
        kept = part[face(0), cs]
        total = reduce_finish(slots1, 0, st)
        norm0[st], bent0[st] = total[0:1], total[1:2]
        alpha0[st] = norm0[st] / bent0[st]
        for f in owned:
            res[face(f), cs] = res[face(f), cs] - alpha0[st] * image[face(f), cs]
        early(st, "n", res, 0, N1_P)
        res[face(0), cs] = res[face(0), cs] - alpha0[st] * (kept + receive(st, S0_P))
        coupled[st] = neumann_late(st, N1_Q)
        c32[st] = restrict(st, res, owned)
    coarse_relay(1, 0)
    for st in sts:
        norm[st] = coupled[st] + schur_early(1, st, zed, N1_P, S1_Q)
        if st + 1 < streams:
            coarse_relay(1, st + 1)
    for st in sts:
        schur_late(st, zed, N1_Q, None)
        reduce_start(slots2, 1, st, [
            norm[st], inner(st, zed, part, every), inner(st, zed, image, owned), jnp.zeros_like(norm[st]),
        ])
    for st in sts:
        cs = columns(st)
        part[face(ls), cs] = part[face(ls), cs] + receive(st, S1_Q)
    for st in sts:
        cs = columns(st)
        total = reduce_finish(slots2, 1, st)
        norm1 = total[0:1]
        beta = norm1 / norm0[st]
        bent1 = total[1:2] + beta * (2.0 * total[2:3] + beta * bent0[st])
        alpha1 = norm1 / bent1
        for f in owned:
            own = pl.ds((f - 1) * nf, nf)
            direction = zed[face(f), cs] + beta * dirn[face(f), cs]
            sol_ref[own, cs] = alpha0[st] * dirn[face(f), cs] + alpha1 * direction
            value = part[face(f), cs] + beta * image[face(f), cs]
            out_ref[own, cs] = res[face(f), cs] - alpha1 * value

    for copy in aux:
        copy.wait_send()
    for st in sts:
        for m in range(MESSAGES):
            message(st, m).wait_send()
        for inst in range(2):
            gather_all(inst, st).wait_send()
            gather_relay(inst, st, core).wait_send()
        reduce_most(slots1, 0, st).wait_send()
        reduce_most(slots2, 1, st).wait_send()


def deliver(sol_ref, res_ref, sol_hbm, res_hbm, sem):
    copies = [
        pltpu.make_async_copy(sol_ref, sol_hbm, sem.at[0]),
        pltpu.make_async_copy(res_ref, res_hbm, sem.at[1]),
    ]
    for copy in copies:
        copy.start()
    for copy in copies:
        copy.wait()


def solution(mesh):
    n = mesh.shape["sub"]

    def shards(right_side, face_weight, schur, neumann, constraint, coarse_inverse):
        ls, nf = face_weight.shape
        rows, r = right_side.shape
        lc = constraint.shape[0]
        ncf = lc // ls
        streams = STREAMS
        cw = r // streams
        extended = rows + nf
        any_spec = pl.BlockSpec(memory_space=pltpu.HBM)
        vmem_spec = pl.BlockSpec(memory_space=pltpu.VMEM)
        results = pl.pallas_call(
            functools.partial(kernel, n, streams),
            name="interface_cg",
            out_shape=(pltpu.VMEM((rows, r), F32),) * 2,
            in_specs=[any_spec] * 6,
            out_specs=(vmem_spec,) * 2,
            scratch_shapes=[
                pltpu.VMEM((ls, nf), F32),
                pltpu.VMEM((ls, nf), F32),
                pltpu.VMEM(schur.shape, BF16),
                pltpu.VMEM(neumann.shape, BF16),
                pltpu.VMEM((lc + ncf, nf), BF16),
                pltpu.VMEM((lc + ncf, coarse_inverse.shape[1]), BF16),
                pltpu.VMEM((ls + 1, nf, cw), F32),
                pltpu.VMEM((extended, r), F32),
                pltpu.VMEM((extended, r), F32),
                pltpu.VMEM((extended, r), F32),
                pltpu.VMEM((extended, r), F32),
                pltpu.VMEM((extended, r), F32),
                pltpu.VMEM((streams, MESSAGES, nf, cw), BF16),
                pltpu.VMEM((streams, MESSAGES, nf, cw), BF16),
                pltpu.VMEM((streams, n // 2, 2, lc, cw), BF16),
                pltpu.VMEM((streams, n // 2, 2, lc, cw), BF16),
                pltpu.VMEM((streams, n, 2, cw), F32),
                pltpu.VMEM((streams, n, 4, cw), F32),
                pltpu.SemaphoreType.DMA((8,)),
                pltpu.SemaphoreType.DMA((3, 2)),
                pltpu.SemaphoreType.DMA((streams, MESSAGES)),
                pltpu.SemaphoreType.DMA((streams, MESSAGES)),
                pltpu.SemaphoreType.DMA((2, streams, 4)),
                pltpu.SemaphoreType.DMA((2, streams, 2)),
            ],
            compiler_params=pltpu.CompilerParams(
                collective_id=0, has_side_effects=True, vmem_limit_bytes=VMEM - 2 * 4 * rows * r - 65536
            ),
        )(right_side, face_weight, schur, neumann, constraint, coarse_inverse)
        return pl.pallas_call(
            deliver,
            name="deliver",
            out_shape=(jax.ShapeDtypeStruct((rows, r), F32),) * 2,
            in_specs=[vmem_spec] * 2,
            out_specs=(any_spec,) * 2,
            scratch_shapes=[pltpu.SemaphoreType.DMA((2,))],
            compiler_params=pltpu.CompilerParams(vmem_limit_bytes=8 * 1024 * 1024),
        )(*results)

    spec = P(("parts", "sub"), None)
    return jax.shard_map(
        shards, mesh=mesh, in_specs=(spec,) * 6, out_specs=(spec, spec), check_vma=False
    )
```

```python
import functools

import jax
import jax.numpy as jnp
from jax import lax
from jax.experimental import pallas as pl
from jax.experimental.pallas import tpu as pltpu
from jax.sharding import PartitionSpec as P

MESH = pl.DeviceIdType.MESH
STREAMS = 2
VMEM = 67043328
F32, BF16 = jnp.float32, jnp.bfloat16

INIT_P, N0_P, N0_Q, S0_P, S0_Q, N1_P, N1_Q, S1_Q = range(8)
MESSAGES = 8


def dot(a, b):
    return jnp.dot(a, b, preferred_element_type=F32)


def dot_first(a, b):
    return lax.dot_general(a, b, (((0,), (0,)), ((), ())), preferred_element_type=F32)


def column_sum(value):
    return jnp.sum(value, axis=0, keepdims=True)


def kernel(
    n, streams,
    rs_hbm, w_hbm, schur_hbm, neumann_hbm, con_hbm, ainv_hbm,
    sol_ref, out_ref,
    w, w_left, schur, neumann, con, ainv, wb,
    res, part, dirn, image, zed,
    sent, came, coarse0, coarse1, slots1, slots2,
    load_sem, aux_sem, msg_send, msg_recv, ag_sem, ar_sem,
):
    ls, nf = w_hbm.shape
    ni = schur_hbm.shape[1]
    ncf = con_hbm.shape[0] // ls
    cw = rs_hbm.shape[1] // streams
    me = lax.axis_index("sub")
    right, left = lax.rem(me + 1, n), lax.rem(me + n - 1, n)
    core, chip = lax.rem(me, 2), me // 2
    partner = chip * 2 + 1 - core

    rest, last = pl.ds(0, (ls - 1) * nf), pl.ds((ls - 1) * nf, nf)
    low, high = pl.ds(0, (ls - 1) * ni), pl.ds((ls - 1) * ni, ni)
    loads = [
        pltpu.make_async_copy(src, dst, load_sem.at[i])
        for i, (src, dst) in enumerate((
            (rs_hbm.at[last], res.at[pl.ds(ls * nf, nf)]),
            (rs_hbm.at[rest], res.at[pl.ds(nf, (ls - 1) * nf)]),
            (con_hbm, con.at[pl.ds(ncf, ls * ncf)]),
            (w_hbm, w),
            (neumann_hbm.at[high], neumann.at[high]),
            (neumann_hbm.at[low], neumann.at[low]),
            (ainv_hbm, ainv.at[pl.ds(ncf, ls * ncf)]),
            (schur_hbm, schur),
        ))
    ]
    for load in loads:
        load.start()

    barrier = pltpu.get_barrier_semaphore()

    def greet(k, carry):
        pl.semaphore_signal(barrier, inc=1, device_id={"sub": lax.rem(me + k, n)}, device_id_type=MESH)
        return carry

    lax.fori_loop(1, n, greet, 0)

    blocks = (coarse0, coarse1)

    def columns(st):
        return pl.ds(st * cw, cw)

    def face(f):
        return pl.ds(f * nf, nf)

    def message(st, m):
        to_right = m in (INIT_P, N0_P, S0_P, N1_P)
        return pltpu.make_async_remote_copy(
            src_ref=sent.at[st, m], dst_ref=came.at[st, m],
            send_sem=msg_send.at[st, m], recv_sem=msg_recv.at[st, m],
            device_id={"sub": right if to_right else left}, device_id_type=MESH,
        )

    def send(st, m, value):
        sent[st, m] = value.astype(BF16)
        message(st, m).start()

    def receive(st, m):
        message(st, m).wait_recv()
        return came[st, m].astype(F32)

    def gather_copy(inst, st, target):
        block = blocks[inst].at[st, chip, core]
        return pltpu.make_async_remote_copy(
            src_ref=block, dst_ref=block, send_sem=ag_sem.at[inst, st, 0], recv_sem=ag_sem.at[inst, st, 1],
            device_id={"sub": target}, device_id_type=MESH,
        )

    def gather_all(inst, st):
        most = blocks[inst].at[st, pl.ds(0, n // 2 - 1), core]
        return pltpu.make_async_remote_copy(
            src_ref=most, dst_ref=most, send_sem=ag_sem.at[inst, st, 0], recv_sem=ag_sem.at[inst, st, 1],
            device_id={"sub": partner}, device_id_type=MESH,
        )

    def gather_relay(inst, st, side):
        half = blocks[inst].at[st, :, side]
        return pltpu.make_async_remote_copy(
            src_ref=half, dst_ref=half, send_sem=ag_sem.at[inst, st, 2], recv_sem=ag_sem.at[inst, st, 3],
            device_id={"sub": partner}, device_id_type=MESH,
        )

    def restrict(st, vector, faces):
        return jnp.concatenate(
            [dot(con[pl.ds(f * ncf, ncf), :], vector[face(f), columns(st)].astype(BF16)) for f in faces], axis=0
        )

    def coarse_start(inst, st, value):
        blocks[inst][st, chip, core] = value.astype(BF16)

    def coarse_send(inst, st):
        def one(k, carry):
            gather_copy(inst, st, lax.rem(me + 2 * k, n)).start()
            return carry

        lax.fori_loop(1, n // 2, one, 0)

    def coarse_relay(inst, st):
        gather_all(inst, st).wait_recv()
        gather_relay(inst, st, core).start()

    def coarse_finish(inst, st):
        gather_relay(inst, st, 1 - core).wait_recv()
        return dot(ainv[...], blocks[inst][st].reshape(-1, cw))

    def reduce_copy(slots, inst, st, target):
        return pltpu.make_async_remote_copy(
            src_ref=slots.at[st, me], dst_ref=slots.at[st, me],
            send_sem=ar_sem.at[inst, st, 0], recv_sem=ar_sem.at[inst, st, 1],
            device_id={"sub": target}, device_id_type=MESH,
        )

    def reduce_most(slots, inst, st):
        most = slots.at[st, pl.ds(0, n - 1)]
        return pltpu.make_async_remote_copy(
            src_ref=most, dst_ref=most, send_sem=ar_sem.at[inst, st, 0], recv_sem=ar_sem.at[inst, st, 1],
            device_id={"sub": partner}, device_id_type=MESH,
        )

    def reduce_start(slots, inst, st, rows):
        slots[st, me] = jnp.concatenate(rows, axis=0)

        def one(k, carry):
            reduce_copy(slots, inst, st, lax.rem(me + k, n)).start()
            return carry

        lax.fori_loop(1, n, one, 0)

    def reduce_finish(slots, inst, st):
        reduce_most(slots, inst, st).wait_recv()
        return jnp.sum(slots[st], axis=0)

    def weighted(kind, f, k, value):
        if kind == "s":
            return value
        return value * (wb[f] if k == 1 else 1.0 - wb[f])

    def operand(st, kind, vector, s, ks):
        parts = [weighted(kind, s + k, k, vector[face(s + k), columns(st)]).astype(BF16) for k in ks]
        return parts[0] if len(parts) == 1 else jnp.concatenate(parts, axis=0)

    def product(kind, s, h, ks, value):
        matrix = neumann if kind == "n" else schur
        block = matrix[pl.ds(s * ni + h * nf, nf), pl.ds(ks[0] * nf, len(ks) * nf)]
        return dot(block, value)

    def early(st, kind, vector, late, m, before=None):
        cs = columns(st)
        order = list(range(ls)) if late == ls else list(range(ls - 1, -1, -1))
        seen = set()
        for s in order:
            if before is not None:
                before(s)
            ks = [k for k in (0, 1) if s + k != late]
            value = operand(st, kind, vector, s, ks)
            for h in (0, 1) if late == ls else (1, 0):
                f = s + h
                term = product(kind, s, h, ks, value)
                if f != late:
                    term = weighted(kind, f, h, term)
                if f in seen:
                    term = part[face(f), cs] + term
                part[face(f), cs] = term
                seen.add(f)
                if m is not None and f == ls - late:
                    send(st, m, term)

    def late_face(st, kind, vector, late, m):
        cs = columns(st)
        s, k = (0, 0) if late == 0 else (ls - 1, 1)
        value = operand(st, kind, vector, s, [k])
        for h in (k, 1 - k):
            f = s + h
            term = product(kind, s, h, [k], value)
            if f == late:
                term = weighted(kind, f, h, part[face(f), cs] + term)
            else:
                term = part[face(f), cs] + weighted(kind, f, h, term)
            part[face(f), cs] = term
            if m is not None and f == late:
                send(st, m, term)

    def inner(st, first, second, faces):
        total = None
        for f in faces:
            term = column_sum(first[face(f), columns(st)] * second[face(f), columns(st)])
            total = term if total is None else total + term
        return total

    every, owned = range(ls + 1), range(1, ls + 1)
    sts = range(streams)

    loads[0].wait()
    for st in sts:
        sent[st, INIT_P] = res[face(ls), columns(st)].astype(BF16)
    loads[1].wait()
    loads[2].wait()
    c32 = {st: restrict(st, res, owned) for st in sts}
    for st in sts:
        coarse_start(0, st, c32[st])
    pl.semaphore_wait(barrier, n - 1)

    last_rows = pl.ds((ls - 1) * ncf, ncf)
    aux = [
        pltpu.make_async_remote_copy(
            src_ref=src, dst_ref=dst, send_sem=aux_sem.at[i, 0], recv_sem=aux_sem.at[i, 1],
            device_id={"sub": right}, device_id_type=MESH,
        )
        for i, (src, dst) in enumerate((
            (w_hbm, w_left),
            (ainv_hbm.at[last_rows], ainv.at[pl.ds(0, ncf)]),
            (con_hbm.at[last_rows], con.at[pl.ds(0, ncf)]),
        ))
    ]
    aux[0].start()
    message(0, INIT_P).start()
    coarse_send(0, 0)
    for st in sts[1:]:
        message(st, INIT_P).start()
    aux[1].start()
    aux[2].start()

    def spread(row):
        return jnp.transpose(jnp.broadcast_to(row, (cw, nf)))

    loads[3].wait()
    for f in range(ls):
        wb[f + 1] = spread(w[pl.ds(f, 1), :])
    loads[4].wait()

    def second_half(st, s):
        if st == 0 and s == ls - 2:
            loads[5].wait()

    def neumann_late(st, m):
        late_face(st, "n", res, 0, m)
        return inner(st, res, part, every)

    def schur_early(inst, st, target, p_message, q_message):
        cs = columns(st)
        x32 = coarse_finish(inst, st)
        if inst == 0:
            x0[st] = x32
        else:
            x32 = x0[st] - alpha0[st] * x32
        x = x32.astype(BF16)
        norm = column_sum(c32[st] * x[ncf:, :].astype(F32))
        for f in every:
            value = part[face(f), cs] + dot_first(con[pl.ds(f * ncf, ncf), :], x[f * ncf : (f + 1) * ncf, :])
            if f == 0:
                value = value + receive(st, p_message)
            target[face(f), cs] = value
        early(st, "s", target, ls, q_message)
        return norm

    def schur_late(st, target, q_arrived, p_message):
        cs = columns(st)
        target[face(ls), cs] = target[face(ls), cs] + receive(st, q_arrived)
        late_face(st, "s", target, ls, p_message)

    x0, alpha0, norm0, bent0, coupled, norm = {}, {}, {}, {}, {}, {}

    for st in sts:
        early(st, "n", res, 0, N0_P, functools.partial(second_half, st))
        if st == 0:
            for each in sts[1:]:
                coarse_send(0, each)
            aux[0].wait_recv()
            wb[0] = spread(w_left[pl.ds(ls - 1, 1), :])
        res[face(0), columns(st)] = receive(st, INIT_P)
        coupled[st] = neumann_late(st, N0_Q)
    coarse_relay(0, 0)
    loads[6].wait()
    aux[1].wait_recv()
    aux[2].wait_recv()
    loads[7].wait()
    for st in sts:
        norm[st] = coupled[st] + schur_early(0, st, dirn, N0_P, S0_Q)
        if st + 1 < streams:
            coarse_relay(0, st + 1)
        schur_late(st, dirn, N0_Q, S0_P)
        reduce_start(slots1, 0, st, [norm[st], inner(st, dirn, part, every)])
    for st in sts:
        cs = columns(st)
        for f in owned:
            value = part[face(f), cs]
            if f == ls:
                value = value + receive(st, S0_Q)
            image[face(f), cs] = value
        coarse_start(1, st, restrict(st, image, owned))
        coarse_send(1, st)
        kept = part[face(0), cs]
        total = reduce_finish(slots1, 0, st)
        norm0[st], bent0[st] = total[0:1], total[1:2]
        alpha0[st] = norm0[st] / bent0[st]
        for f in owned:
            res[face(f), cs] = res[face(f), cs] - alpha0[st] * image[face(f), cs]
        early(st, "n", res, 0, N1_P)
        res[face(0), cs] = res[face(0), cs] - alpha0[st] * (kept + receive(st, S0_P))
        coupled[st] = neumann_late(st, N1_Q)
        c32[st] = restrict(st, res, owned)
    coarse_relay(1, 0)
    for st in sts:
        norm[st] = coupled[st] + schur_early(1, st, zed, N1_P, S1_Q)
        if st + 1 < streams:
            coarse_relay(1, st + 1)
        schur_late(st, zed, N1_Q, None)
        reduce_start(slots2, 1, st, [
            norm[st], inner(st, zed, part, every), inner(st, zed, image, owned), jnp.zeros_like(norm[st]),
        ])
    for st in sts:
        cs = columns(st)
        part[face(ls), cs] = part[face(ls), cs] + receive(st, S1_Q)
    for st in sts:
        cs = columns(st)
        total = reduce_finish(slots2, 1, st)
        norm1 = total[0:1]
        beta = norm1 / norm0[st]
        bent1 = total[1:2] + beta * (2.0 * total[2:3] + beta * bent0[st])
        alpha1 = norm1 / bent1
        for f in owned:
            own = pl.ds((f - 1) * nf, nf)
            direction = zed[face(f), cs] + beta * dirn[face(f), cs]
            sol_ref[own, cs] = alpha0[st] * dirn[face(f), cs] + alpha1 * direction
            value = part[face(f), cs] + beta * image[face(f), cs]
            out_ref[own, cs] = res[face(f), cs] - alpha1 * value

    for copy in aux:
        copy.wait_send()
    for st in sts:
        for m in range(MESSAGES):
            message(st, m).wait_send()
        for inst in range(2):
            gather_all(inst, st).wait_send()
            gather_relay(inst, st, core).wait_send()
        reduce_most(slots1, 0, st).wait_send()
        reduce_most(slots2, 1, st).wait_send()


def deliver(sol_ref, res_ref, sol_hbm, res_hbm, sem):
    copies = [
        pltpu.make_async_copy(sol_ref, sol_hbm, sem.at[0]),
        pltpu.make_async_copy(res_ref, res_hbm, sem.at[1]),
    ]
    for copy in copies:
        copy.start()
    for copy in copies:
        copy.wait()


def solution(mesh):
    n = mesh.shape["sub"]

    def shards(right_side, face_weight, schur, neumann, constraint, coarse_inverse):
        ls, nf = face_weight.shape
        rows, r = right_side.shape
        lc = constraint.shape[0]
        ncf = lc // ls
        streams = STREAMS
        cw = r // streams
        extended = rows + nf
        any_spec = pl.BlockSpec(memory_space=pltpu.HBM)
        vmem_spec = pl.BlockSpec(memory_space=pltpu.VMEM)
        results = pl.pallas_call(
            functools.partial(kernel, n, streams),
            name="interface_cg",
            out_shape=(pltpu.VMEM((rows, r), F32),) * 2,
            in_specs=[any_spec] * 6,
            out_specs=(vmem_spec,) * 2,
            scratch_shapes=[
                pltpu.VMEM((ls, nf), F32),
                pltpu.VMEM((ls, nf), F32),
                pltpu.VMEM(schur.shape, BF16),
                pltpu.VMEM(neumann.shape, BF16),
                pltpu.VMEM((lc + ncf, nf), BF16),
                pltpu.VMEM((lc + ncf, coarse_inverse.shape[1]), BF16),
                pltpu.VMEM((ls + 1, nf, cw), F32),
                pltpu.VMEM((extended, r), F32),
                pltpu.VMEM((extended, r), F32),
                pltpu.VMEM((extended, r), F32),
                pltpu.VMEM((extended, r), F32),
                pltpu.VMEM((extended, r), F32),
                pltpu.VMEM((streams, MESSAGES, nf, cw), BF16),
                pltpu.VMEM((streams, MESSAGES, nf, cw), BF16),
                pltpu.VMEM((streams, n // 2, 2, lc, cw), BF16),
                pltpu.VMEM((streams, n // 2, 2, lc, cw), BF16),
                pltpu.VMEM((streams, n, 2, cw), F32),
                pltpu.VMEM((streams, n, 4, cw), F32),
                pltpu.SemaphoreType.DMA((8,)),
                pltpu.SemaphoreType.DMA((3, 2)),
                pltpu.SemaphoreType.DMA((streams, MESSAGES)),
                pltpu.SemaphoreType.DMA((streams, MESSAGES)),
                pltpu.SemaphoreType.DMA((2, streams, 4)),
                pltpu.SemaphoreType.DMA((2, streams, 2)),
            ],
            compiler_params=pltpu.CompilerParams(
                collective_id=0, has_side_effects=True, vmem_limit_bytes=VMEM - 2 * 4 * rows * r - 65536
            ),
        )(right_side, face_weight, schur, neumann, constraint, coarse_inverse)
        return pl.pallas_call(
            deliver,
            name="deliver",
            out_shape=(jax.ShapeDtypeStruct((rows, r), F32),) * 2,
            in_specs=[vmem_spec] * 2,
            out_specs=(any_spec,) * 2,
            scratch_shapes=[pltpu.SemaphoreType.DMA((2,))],
            compiler_params=pltpu.CompilerParams(vmem_limit_bytes=8 * 1024 * 1024),
        )(*results)

    spec = P(("parts", "sub"), None)
    return jax.shard_map(
        shards, mesh=mesh, in_specs=(spec,) * 6, out_specs=(spec, spec), check_vma=False
    )
```
